32 devices in a mesh: win: 8 (over z, y), seq: 4 (over x, core).
Axes of the slice: x: 2, y: 2, z: 4, core: 2. Of those that a mesh axis runs over, the one named last changes fastest.
Arguments:
- queries: bfloat16 [2, 8, 2048, 2048], P(None, 'win', 'seq'), may hold values from -4.5 to 4.5
- key_states: bfloat16 [2, 8, 2048, 2048], P(None, 'win', 'seq'), may hold values from -4.5 to 4.5
- value_states: bfloat16 [2, 8, 2048, 2048], P(None, 'win', 'seq'), may hold values from -5 to 5
- out_grad: bfloat16 [2, 8, 2048, 2048], P(None, 'win', 'seq'), may hold values from -60 to 60
Outputs:
- query_grad: bfloat16 [2, 8, 2048, 2048], P(None, 'win', 'seq')
- key_grad: bfloat16 [2, 8, 2048, 2048], P(None, 'win', 'seq')
- value_grad: bfloat16 [2, 8, 2048, 2048], P(None, 'win', 'seq')
The draws below stay inside these ranges and needn't reach their ends.
All inputs are finite; a program needn't handle non-finite values.
Results may differ from the reference program's by a relative error of at most 0.0095.
Values may be sent and summed in bfloat16 or wider, within the bound.
No kernel may reach another device: no remote copies, remote signals or barrier semaphores. Data moves between devices by JAX's collectives and lax.ppermute only.
A program may use at most 192 MiB of HBM per device.

```python
import jax
import jax.numpy as jnp
from jax import lax

HEADS = 16
HDIM = 128
D = 2048
ROWS = 32
COLS = 64
WTOK = 2048
SAMPLES = 2
WINDOWS = 8


def rough_base(key, salt):
    values = jax.random.normal(jax.random.fold_in(key, salt), (SAMPLES, WINDOWS, WTOK, D), jnp.float32)
    values = jnp.clip(values, -4.5, 4.5)
    return values


def draw_queries(key, part):
    values = rough_base(key, 11)
    return values.astype(jnp.bfloat16)


def draw_key_states(key, part):
    values = rough_base(key, 13)
    return values.astype(jnp.bfloat16)


def block_levels(rng, dims, pieces, low, top_value):
    level = 1.0
    for dim, parts in pieces:
        heights = jax.random.uniform(jax.random.fold_in(jax.random.fold_in(rng, 6), dim), (parts,), jnp.float32, low / len(pieces), top_value / len(pieces))
        level = level * jnp.repeat(jnp.exp(heights), dims[dim] // parts).reshape((-1,) + (1,) * (len(dims) - 1 - dim))
    return level


def scatter_about(key, extent, deviation, limit, cuts=(), held_as=jnp.bfloat16):
    entries = jax.random.normal(key, extent, jnp.float32) * deviation
    if len(cuts) > 0:
        entries = block_levels(key, extent, cuts, -0.22, 0.18) * entries
    return jnp.clip(entries, min=-limit, max=limit).astype(held_as)


def setup_inputs(seed: int = 0) -> dict:
    seeds = jax.random.split(jax.random.key(seed), 5)
    queries = draw_queries(jax.random.fold_in(seeds[4], 71), 0)
    key_states = draw_key_states(jax.random.fold_in(seeds[4], 71), 0)
    value_states = scatter_about(seeds[2], (SAMPLES, WINDOWS, WTOK, D), 1.0, 5.0, ((1, 8), (2, 4)))
    out_grad = scatter_about(seeds[3], (SAMPLES, WINDOWS, WTOK, D), 12.0, 60.0, ((1, 8), (2, 4)))
    return dict(queries=queries, key_states=key_states, value_states=value_states, out_grad=out_grad)


def to_grid(values, windows):
    samples = values.shape[0]
    shaped = values.reshape(samples, windows, ROWS, COLS, -1)
    return shaped.transpose(0, 2, 1, 3, 4).reshape(samples, ROWS, windows * COLS, -1)


def to_windows(token_grid, windows):
    samples = token_grid.shape[0]
    shaped = token_grid.reshape(samples, ROWS, windows, COLS, -1)
    return shaped.transpose(0, 2, 1, 3, 4).reshape(samples, windows, ROWS * COLS, -1)


def window_grads(query_heads, key_heads, value_heads, grad_heads):
    samples_here, tokens, own_heads, head_size = query_heads.shape
    block_rows = min(512, tokens)
    factor = head_size ** -0.5
    query_wide = query_heads.astype(jnp.float32)
    key_wide = key_heads.astype(jnp.float32)
    value_wide = value_heads.astype(jnp.float32)
    grad_wide = grad_heads.astype(jnp.float32)

    def one_block(totals, offset):
        key_total, value_total = totals
        query_block = lax.dynamic_slice_in_dim(query_wide, offset, block_rows, 1)
        grad_block = lax.dynamic_slice_in_dim(grad_wide, offset, block_rows, 1)
        scores = jnp.einsum("bqhd,bkhd->bhqk", query_block, key_wide) * factor
        scores = scores - jnp.max(scores, axis=3, keepdims=True)
        weights = jnp.exp(scores)
        weights = weights / jnp.sum(weights, axis=3, keepdims=True)
        weights_low = weights.astype(jnp.bfloat16).astype(jnp.float32)
        value_total = value_total + jnp.einsum("bhqk,bqhd->bkhd", weights_low, grad_block)
        grad_probs = jnp.einsum("bqhd,bkhd->bhqk", grad_block, value_wide)
        row_dot = jnp.sum(weights * grad_probs, axis=3, keepdims=True)
        grad_scores = (weights * (grad_probs - row_dot) * factor).astype(jnp.bfloat16).astype(jnp.float32)
        query_block_grad = jnp.einsum("bhqk,bkhd->bqhd", grad_scores, key_wide).astype(jnp.bfloat16)
        key_total = key_total + jnp.einsum("bhqk,bqhd->bkhd", grad_scores, query_block)
        return (key_total, value_total), query_block_grad

    starts = jnp.arange(tokens // block_rows, dtype=jnp.int32) * block_rows
    zero_acc = jnp.zeros(query_heads.shape, jnp.float32)
    (key_total, value_total), query_blocks = lax.scan(one_block, (zero_acc, zero_acc), starts)
    query_grad = jnp.moveaxis(query_blocks, 0, 1).reshape(samples_here, tokens, own_heads, head_size)
    return jnp.stack([query_grad, key_total.astype(jnp.bfloat16), value_total.astype(jnp.bfloat16)])


def reference(queries, key_states, value_states, out_grad):
    samples = queries.shape[0]
    windows = queries.shape[1]
    moved_grad = to_windows(jnp.roll(to_grid(out_grad, windows), (-(ROWS // 2), -(COLS // 2)), axis=(1, 2)), windows)

    def as_items(values):
        return values.reshape(samples * windows, 1, ROWS * COLS, HEADS, HDIM)

    def one_window(inputs):
        return window_grads(inputs[0], inputs[1], inputs[2], inputs[3])

    stacked = lax.map(one_window, (as_items(queries), as_items(key_states), as_items(value_states), as_items(moved_grad)))

    def restore(which):
        shifted = stacked[:, which].reshape(samples, windows, ROWS * COLS, HEADS * HDIM)
        return to_windows(jnp.roll(to_grid(shifted, windows), (ROWS // 2, COLS // 2), axis=(1, 2)), windows)

    return restore(0), restore(1), restore(2)
```

```python
import functools
import math

import jax
import jax.numpy as jnp
from jax import lax
from jax.experimental import pallas as pl
from jax.experimental.pallas import tpu as pltpu
from jax.sharding import PartitionSpec as P

HDIM = 128
COLS = 64
HALF = COLS // 2
UNITS = 2


def exchanged(block, across, west):
    wins, seqs = lax.axis_size("win"), lax.axis_size("seq")
    route = [
        (w * seqs + s, ((w - west) % wins) * seqs + (s ^ across))
        for w in range(wins)
        for s in range(seqs)
    ]
    return lax.ppermute(block, ("win", "seq"), route)


def cost(flops, read, exps=0):
    return pl.CostEstimate(flops=int(flops), bytes_accessed=int(read), transcendentals=int(exps))


def head_block(rows, cols, width, sample, col, across, share):
    return pl.BlockSpec(
        (1, 1, rows, cols, width),
        lambda u, me: (sample, 0, 0, col, (me[0] ^ across) * share + u),
    )


def packed(args, me, sample, first, units, heads_each, seqs):
    queries, _, _, out_grad = args
    rows = queries.shape[2]
    tokens, part = rows * COLS, rows * HALF
    width = units * HDIM
    share = heads_each // units
    here = [k for k in range(seqs) if k]
    everyone = list(range(seqs))

    def kernel(me_ref, *refs):
        ins, outs = refs[: 3 * len(here) + 2 * seqs - 1], refs[3 * len(here) + 2 * seqs - 1 :]
        for i in range(len(here)):
            for n in range(3):
                outs[i][n * tokens : (n + 1) * tokens] = ins[4 * i + n][0, 0].reshape(tokens, width)
            outs[i][3 * tokens :] = ins[4 * i + 3][0, 0].reshape(part, width)
        for i in range(seqs):
            outs[len(here) + i][...] = ins[4 * len(here) + i][0, 0].reshape(part, width)

    offset = first // units
    specs, operands = [], []
    for k in here:
        for n in range(3):
            specs.append(
                pl.BlockSpec(
                    (1, 1, rows, COLS, width),
                    lambda u, m, k=k: (sample, 0, 0, 0, (m[0] ^ k) * share + offset),
                )
            )
            operands.append(args[n])
        specs.append(
            pl.BlockSpec(
                (1, 1, rows, HALF, width),
                lambda u, m, k=k: (sample, 0, 0, 1, (m[0] ^ k) * share + offset),
            )
        )
        operands.append(out_grad)
    for k in everyone:
        specs.append(
            pl.BlockSpec(
                (1, 1, rows, HALF, width),
                lambda u, m, k=k: (sample, 0, 0, 0, (m[0] ^ k) * share + offset),
            )
        )
        operands.append(out_grad)
    sizes = [3 * tokens + part] * len(here) + [part] * seqs
    shapes = [jax.ShapeDtypeStruct((n, width), jnp.bfloat16) for n in sizes]
    out = pl.pallas_call(
        kernel,
        grid_spec=pltpu.PrefetchScalarGridSpec(
            num_scalar_prefetch=1,
            grid=(1,),
            in_specs=specs,
            out_specs=[pl.BlockSpec((n, width), lambda u, m: (0, 0)) for n in sizes],
        ),
        out_shape=shapes,
        name="pack",
        cost_estimate=cost(0, 4 * sum(sizes) * width),
    )(me, *operands)
    return dict(zip(here, out[: len(here)])), dict(zip(everyone, out[len(here) :]))


def window_grads(args, me, sample, first, units, heads_each, seqs, arrived, arrived_west):
    rows = args[0].shape[2]
    tokens, part = rows * COLS, rows * HALF
    total = tokens * seqs
    block = min(256, total)
    turned = seqs // 2
    here = [k for k in range(seqs) if k]
    factor = HDIM ** (-0.5)
    slope = factor * math.log2(math.e)

    def kernel(me_ref, q_own, k_own, v_own, g_own, *refs):
        got = refs[: len(here)]
        got_west = refs[len(here) : len(here) + seqs]
        outs = refs[len(here) + seqs : len(here) + 3 * seqs]
        qs, ks, vs, gs, kt, dq, dk, dv = refs[len(here) + 3 * seqs :]

        for n, (own, held) in enumerate(((q_own, qs), (k_own, ks), (v_own, vs))):
            held[0:tokens] = own[0, 0].reshape(tokens, HDIM)
            for i, k in enumerate(here):
                held[k * tokens : (k + 1) * tokens] = got[i][n * tokens : (n + 1) * tokens]
        for k in range(seqs):
            near = g_own[0, 0] if k == 0 else got[k - 1][3 * tokens :].reshape(rows, HALF, HDIM)
            far = got_west[k][...].reshape(rows, HALF, HDIM)
            at = (k ^ turned) * tokens
            gs[at : at + tokens] = jnp.concatenate([near, far], axis=1).reshape(tokens, HDIM)
        kt[...] = ks[...].T
        dk[...] = jnp.zeros_like(dk)
        dv[...] = jnp.zeros_like(dv)

        def step(i, carry):
            at = pl.ds(pl.multiple_of(i * block, block), block)
            query, grad = qs[at, :], gs[at, :]
            scores = lax.dot_general(
                ks[...], query, (((1,), (1,)), ((), ())), preferred_element_type=jnp.float32
            )
            top = jnp.max(scores, axis=0, keepdims=True) * slope
            weights = jnp.exp2(scores * slope - top)
            weights = weights * (1.0 / jnp.sum(weights, axis=0, keepdims=True))
            dv[...] += jnp.dot(
                weights.astype(jnp.bfloat16), grad, preferred_element_type=jnp.float32
            )
            grad_probs = lax.dot_general(
                vs[...], grad, (((1,), (1,)), ((), ())), preferred_element_type=jnp.float32
            )
            row_dot = jnp.sum(weights * grad_probs, axis=0, keepdims=True)
            grad_scores = (weights * (grad_probs - row_dot)).astype(jnp.bfloat16)
            dk[...] += jnp.dot(grad_scores, query, preferred_element_type=jnp.float32)
            turned_grad = jnp.dot(kt[...], grad_scores, preferred_element_type=jnp.float32)
            dq[at, :] = (turned_grad.T * factor).astype(jnp.bfloat16)
            return carry

        lax.fori_loop(0, total // block, step, 0)

        for k in range(seqs):
            at = pl.ds((k ^ turned) * tokens, tokens)
            for n, held in enumerate((dq, dk, dv)):
                value = held[at, :]
                if n == 1:
                    value = value * factor
                value = value.astype(jnp.bfloat16).reshape(rows, COLS, HDIM)
                to = pl.ds(n * part, part)
                outs[k][to, :] = value[:, :HALF].reshape(part, HDIM)
                outs[seqs + k][to, :] = value[:, HALF:].reshape(part, HDIM)

    own = [
        pl.BlockSpec(
            (1, 1, rows, COLS, HDIM), lambda u, m: (sample, 0, 0, 0, m[0] * heads_each + first + u)
        )
    ] * 3 + [
        pl.BlockSpec(
            (1, 1, rows, HALF, HDIM), lambda u, m: (sample, 0, 0, 1, m[0] * heads_each + first + u)
        )
    ]
    full, small = 3 * tokens + part, part
    got = [pl.BlockSpec((full, HDIM), lambda u, m: (0, u))] * len(here)
    got_west = [pl.BlockSpec((small, HDIM), lambda u, m: (0, u))] * seqs
    out_rows = 3 * part
    held = pltpu.VMEM((total, HDIM), jnp.bfloat16)
    wide = pltpu.VMEM((total, HDIM), jnp.float32)
    out = pl.pallas_call(
        kernel,
        grid_spec=pltpu.PrefetchScalarGridSpec(
            num_scalar_prefetch=1,
            grid=(units,),
            in_specs=own + got + got_west,
            out_specs=[pl.BlockSpec((out_rows, HDIM), lambda u, m: (0, u))] * (2 * seqs),
            scratch_shapes=[held] * 4
            + [pltpu.VMEM((HDIM, total), jnp.bfloat16), held, wide, wide],
        ),
        out_shape=[jax.ShapeDtypeStruct((out_rows, units * HDIM), jnp.bfloat16)] * (2 * seqs),
        compiler_params=pltpu.CompilerParams(vmem_limit_bytes=48 * 2**20),
        name="grads",
        cost_estimate=cost(
            units * 10 * total * total * HDIM, units * 14 * total * HDIM, units * total * total
        ),
    )(
        me,
        *args,
        *[arrived[k] for k in here],
        *[arrived_west[k] for k in range(seqs)],
    )
    return out[:seqs], out[seqs:]


def placed(results, me, shape, sample, first, units, heads_each, seqs, stayed, came):
    rows = shape[2]
    part = rows * HALF
    width = units * HDIM
    share = heads_each // units
    offset = first // units

    def kernel(me_ref, *refs):
        stay, come = refs[:seqs], refs[seqs : 2 * seqs]
        outs = refs[-3:]
        for k in range(seqs):

            @pl.when(pl.program_id(0) == k)
            def _():
                for n in range(3):
                    outs[n][0, 0, :, :HALF] = come[k][n * part : (n + 1) * part].reshape(
                        rows, HALF, width
                    )
                    outs[n][0, 0, :, HALF:] = stay[k][n * part : (n + 1) * part].reshape(
                        rows, HALF, width
                    )

    piece = pl.BlockSpec((3 * part, width), lambda k, m: (0, 0))
    kept = [pl.BlockSpec(memory_space=pl.ANY)] * len(results)
    return pl.pallas_call(
        kernel,
        grid_spec=pltpu.PrefetchScalarGridSpec(
            num_scalar_prefetch=1,
            grid=(seqs,),
            in_specs=[piece] * (2 * seqs) + kept,
            out_specs=[
                pl.BlockSpec(
                    (1, 1, rows, COLS, width),
                    lambda k, m: (sample, 0, 0, 0, (m[0] ^ k) * share + offset),
                )
            ]
            * 3,
        ),
        out_shape=[jax.ShapeDtypeStruct(shape, jnp.bfloat16)] * 3,
        input_output_aliases={1 + 2 * seqs + i: i for i in range(len(results))},
        name="place",
        cost_estimate=cost(0, 4 * 6 * seqs * part * width),
    )(me, *stayed, *came, *results)


def on_device(*args):
    samples, _, local_tokens, model_width = args[0].shape
    seqs = lax.axis_size("seq")
    heads_each = model_width // HDIM // seqs
    rows = local_tokens // COLS
    me = lax.axis_index("seq").astype(jnp.int32).reshape(1)
    args = [a.reshape(samples, 1, rows, COLS, model_width) for a in args]
    shape = args[0].shape
    units = math.gcd(UNITS, heads_each)
    chunks = [(s, f) for s in range(samples) for f in range(0, heads_each, units)]
    order = sorted(range(seqs), key=lambda k: -k)

    moving = []
    for sample, first in chunks:
        near, far = packed(args, me, sample, first, units, heads_each, seqs)
        got = {k: exchanged(near[k], k, 0) for k in order if k}
        got_west = {k: exchanged(far[k], k, 1) for k in order}
        moving.append((got, got_west))
    leaving = []
    for (sample, first), (got, got_west) in zip(chunks, moving):
        stay, east = window_grads(
            args, me, sample, first, units, heads_each, seqs, got, got_west
        )
        stayed = {k: exchanged(stay[k], k, 0) if k else stay[k] for k in order}
        came = {k: exchanged(east[k], k, -1) for k in order}
        leaving.append((stayed, came))
    results = []
    for (sample, first), (stayed, came) in zip(chunks, leaving):
        results = placed(
            results,
            me,
            shape,
            sample,
            first,
            units,
            heads_each,
            seqs,
            [stayed[k] for k in range(seqs)],
            [came[k] for k in range(seqs)],
        )
    return tuple(r.reshape(samples, 1, local_tokens, model_width) for r in results)


def solution(mesh):
    spec = P(None, "win", "seq", None)
    return jax.shard_map(
        on_device,
        mesh=mesh,
        in_specs=(spec,) * 4,
        out_specs=(spec,) * 3,
        check_vma=False,
    )
```

```python
import functools
import math

import jax
import jax.numpy as jnp
from jax import lax
from jax.experimental import pallas as pl
from jax.experimental.pallas import tpu as pltpu
from jax.sharding import PartitionSpec as P


HDIM = 128
COLS = 64
HALF = COLS // 2
UNITS = 2


def exchanged(block, across, west):
    wins, seqs = lax.axis_size("win"), lax.axis_size("seq")
    route = [
        (w * seqs + s, ((w - west) % wins) * seqs + (s ^ across))
        for w in range(wins)
        for s in range(seqs)
    ]
    return lax.ppermute(block, ("win", "seq"), route)


def cost(flops, read, exps=0):
    return pl.CostEstimate(flops=int(flops), bytes_accessed=int(read), transcendentals=int(exps))


def packed(arrays, me, sample, first, units, heads_each, peers):
    rows = arrays[0][0].shape[2]
    width = units * HDIM
    share, offset = heads_each // units, first // units
    sizes = [rows * (COLS if half is None else HALF) for _, half in arrays]
    count = len(arrays)

    def kernel(me_ref, *refs):
        for i in range(len(peers)):
            out, at = refs[i - len(peers)], 0
            for piece, size in zip(refs[i * count :], sizes):
                out[at : at + size] = piece[0, 0].reshape(size, width)
                at += size

    specs = [
        pl.BlockSpec(
            (1, 1, rows, COLS if half is None else HALF, width),
            lambda u, m, k=k, half=half: (sample, 0, 0, half or 0, (m[0] ^ k) * share + offset),
        )
        for k in peers
        for _, half in arrays
    ]
    out = pl.pallas_call(
        kernel,
        grid_spec=pltpu.PrefetchScalarGridSpec(
            num_scalar_prefetch=1,
            grid=(1,),
            in_specs=specs,
            out_specs=[pl.BlockSpec((sum(sizes), width), lambda u, m: (0, 0))] * len(peers),
        ),
        out_shape=[jax.ShapeDtypeStruct((sum(sizes), width), jnp.bfloat16)] * len(peers),
        name="pack",
        cost_estimate=cost(0, 4 * sum(sizes) * width * len(peers)),
    )(me, *[a for _ in peers for a, _ in arrays])
    return dict(zip(peers, out))


def window_grads(args, me, sample, first, units, heads_each, seqs, arrived, arrived_west):
    rows = args[0].shape[2]
    tokens, part = rows * COLS, rows * HALF
    total = tokens * seqs
    block, slab = min(512, total), min(256, total)
    turned = seqs // 2
    here = [k for k in range(seqs) if k]
    factor = HDIM ** (-0.5)
    slope = factor * math.log2(math.e)

    def product(a, b, i, j):
        return lax.dot_general(a, b, (((i,), (j,)), ((), ())), preferred_element_type=jnp.float32)

    def folded(reduce, x):
        return reduce(x.reshape(-1, 8, x.shape[1]), axis=0)

    def kernel(me_ref, q_own, k_own, v_own, g_own, *refs):
        got = refs[: len(here)]
        got_west = refs[len(here) : len(here) + seqs]
        outs = refs[-8 - 2 * seqs : -8]
        qs, ks, vs, gs, kt, dq, dk, dv = refs[-8:]

        for n, (own, held) in enumerate(((q_own, qs), (k_own, ks), (v_own, vs))):
            held[0:tokens] = own[0, 0].reshape(tokens, HDIM)
            for i, k in enumerate(here):
                held[k * tokens : (k + 1) * tokens] = got[i][n * tokens : (n + 1) * tokens]
        for k in range(seqs):
            near = g_own[0, 0] if k == 0 else got[k - 1][3 * tokens :].reshape(rows, HALF, HDIM)
            far = got_west[k][...].reshape(rows, HALF, HDIM)
            at = (k ^ turned) * tokens
            gs[at : at + tokens] = jnp.concatenate([near, far], axis=1).reshape(tokens, HDIM)
        kt[...] = ks[...].T
        dk[...] = jnp.zeros_like(dk)
        dv[...] = jnp.zeros_like(dv)

        def step(i, carry):
            at = pl.ds(pl.multiple_of(i * block, block), block)
            query, grad = qs[at, :], gs[at, :]
            slabs = [slice(j, j + slab) for j in range(0, total, slab)]
            scores = [product(ks[j, :], query, 1, 1) for j in slabs]
            top = functools.reduce(jnp.maximum, [folded(jnp.max, x) for x in scores])
            top = jnp.max(top, axis=0, keepdims=True) * slope
            weights = [jnp.exp2(x * slope - top) for x in scores]
            grad_probs = [product(vs[j, :], grad, 1, 1) for j in slabs]
            mass = sum(folded(jnp.sum, w) for w in weights)
            dots = sum(folded(jnp.sum, w * g) for w, g in zip(weights, grad_probs))
            scale = 1.0 / jnp.sum(mass, axis=0, keepdims=True)
            row_dot = jnp.sum(dots, axis=0, keepdims=True) * scale
            column = scale.T
            grad = (grad.astype(jnp.float32) * column).astype(jnp.bfloat16)
            query = (query.astype(jnp.float32) * (column * factor)).astype(jnp.bfloat16)
            turned_grad = 0.0
            for j, w, g in zip(slabs, weights, grad_probs):
                dv[j, :] += product(w.astype(jnp.bfloat16), grad, 1, 0)
                u = (w * (g - row_dot)).astype(jnp.bfloat16)
                dk[j, :] += product(u, query, 1, 0)
                turned_grad += product(kt[:, j], u, 1, 0)
            dq[at, :] = (turned_grad * (scale * factor)).T.astype(jnp.bfloat16)
            return carry

        lax.fori_loop(0, total // block, step, 0)

        for k in range(seqs):
            at = pl.ds((k ^ turned) * tokens, tokens)
            for n, held in enumerate((dq, dk, dv)):
                value = held[at, :]
                value = value.astype(jnp.bfloat16).reshape(rows, COLS, HDIM)
                to = pl.ds(n * part, part)
                outs[k][to, :] = value[:, :HALF].reshape(part, HDIM)
                outs[seqs + k][to, :] = value[:, HALF:].reshape(part, HDIM)

    own = [
        pl.BlockSpec(
            (1, 1, rows, COLS, HDIM), lambda u, m: (sample, 0, 0, 0, m[0] * heads_each + first + u)
        )
    ] * 3 + [
        pl.BlockSpec(
            (1, 1, rows, HALF, HDIM), lambda u, m: (sample, 0, 0, 1, m[0] * heads_each + first + u)
        )
    ]
    full, small = 3 * tokens + part, part
    got = [pl.BlockSpec((full, HDIM), lambda u, m: (0, u))] * len(here)
    got_west = [pl.BlockSpec((small, HDIM), lambda u, m: (0, first + u))] * seqs
    out_rows = 3 * part
    held = pltpu.VMEM((total, HDIM), jnp.bfloat16)
    wide = pltpu.VMEM((total, HDIM), jnp.float32)
    out = pl.pallas_call(
        kernel,
        grid_spec=pltpu.PrefetchScalarGridSpec(
            num_scalar_prefetch=1,
            grid=(units,),
            in_specs=own + got + got_west,
            out_specs=[pl.BlockSpec((out_rows, HDIM), lambda u, m: (0, u))] * (2 * seqs),
            scratch_shapes=[held] * 4
            + [pltpu.VMEM((HDIM, total), jnp.bfloat16), held, wide, wide],
        ),
        out_shape=[jax.ShapeDtypeStruct((out_rows, units * HDIM), jnp.bfloat16)] * (2 * seqs),
        compiler_params=pltpu.CompilerParams(vmem_limit_bytes=48 * 2**20),
        name="grads",
        cost_estimate=cost(
            units * 10 * total * total * HDIM, units * 14 * total * HDIM, units * total * total
        ),
    )(
        me,
        *args,
        *[arrived[k] for k in here],
        *[arrived_west[k] for k in range(seqs)],
    )
    return out[:seqs], out[seqs:]


def placed(results, me, shape, sample, first, units, heads_each, pieces):
    rows = shape[2]
    width = units * HDIM
    share, offset = heads_each // units, first // units

    def kernel(me_ref, *refs):
        outs, sems = refs[-4:-1], refs[-1]
        copies = []
        for i, (k, column, _) in enumerate(pieces):
            head = pl.multiple_of(((me_ref[0] ^ k) * share + offset) * width, width)
            for n in range(3):
                to = outs[n].at[sample, 0, :, pl.ds(column, HALF), pl.ds(head, width)]
                copies.append(pltpu.make_async_copy(refs[i].at[n], to, sems.at[i, n]))
        for copy in copies:
            copy.start()
        for copy in copies:
            copy.wait()

    block = (3, rows, HALF, width)
    kept = [pl.BlockSpec(memory_space=pl.ANY)] * len(results)
    return pl.pallas_call(
        kernel,
        grid_spec=pltpu.PrefetchScalarGridSpec(
            num_scalar_prefetch=1,
            grid=(1,),
            in_specs=[pl.BlockSpec(block, lambda k, m: (0, 0, 0, 0))] * len(pieces) + kept,
            out_specs=[pl.BlockSpec(memory_space=pl.ANY)] * 3,
            scratch_shapes=[pltpu.SemaphoreType.DMA((len(pieces), 3))],
        ),
        out_shape=[jax.ShapeDtypeStruct(shape, jnp.bfloat16)] * 3,
        input_output_aliases={1 + len(pieces) + i: i for i in range(len(results))},
        name="place",
        cost_estimate=cost(0, 4 * math.prod(block) * len(pieces)),
    )(me, *[x.reshape(block) for _, _, x in pieces], *results)


def on_device(*args):
    samples, _, local_tokens, model_width = args[0].shape
    seqs = lax.axis_size("seq")
    heads_each = model_width // HDIM // seqs
    rows = local_tokens // COLS
    me = lax.axis_index("seq").astype(jnp.int32).reshape(1)
    args = [a.reshape(samples, 1, rows, COLS, model_width) for a in args]
    shape = args[0].shape
    turned = seqs // 2
    crossing, beside = list(range(turned, seqs)), list(range(turned))
    units = math.gcd(UNITS, heads_each)
    chunks = [(n, f) for n in range(samples) for f in range(0, heads_each, units)]

    near = [(args[0], None), (args[1], None), (args[2], None), (args[3], 1)]
    moving, got_west, step = [], {}, 0

    def sent(arrays, place, peers, west):
        nonlocal step
        step += 1
        blocks = packed(arrays, me, *place, peers)
        return {k: exchanged(blocks[k], k, west) for k in peers}

    for sample, first in chunks:
        at = (sample, first, units, heads_each)
        got = {}
        if not moving:
            for k in crossing:
                got.update(sent(near, at, [k], 0))
        else:
            got.update(sent(near, at, crossing + beside[1:], 0))
        if sample not in got_west:
            whole = (sample, 0, heads_each, heads_each)
            got_west[sample] = sent([(args[3], 0)], whole, beside + crossing, 1)
        if not moving and beside[1:]:
            got.update(sent(near, at, beside[1:], 0))
        moving.append(got)
    leaving = []
    for (sample, first), got in zip(chunks, moving):
        stay, east = window_grads(
            args, me, sample, first, units, heads_each, seqs, got, got_west[sample]
        )
        came = {k: exchanged(east[k], k, -1) for k in crossing + beside}
        stayed = {k: exchanged(stay[k], k, 0) if k else stay[k] for k in crossing + beside}
        leaving.append((stayed, came))
    results = []
    for i, ((sample, first), (stayed, came)) in enumerate(zip(chunks, leaving)):
        early = [(k, HALF, stayed[k]) for k in beside] + [(k, 0, came[k]) for k in beside]
        late = [(k, 0, came[k]) for k in crossing]
        last = [(k, HALF, stayed[k]) for k in crossing]
        for pieces in [early, late, last] if i == len(chunks) - 1 else [early + late + last]:
            results = placed(results, me, shape, sample, first, units, heads_each, pieces)
    return tuple(r.reshape(samples, 1, local_tokens, model_width) for r in results)


def solution(mesh):
    spec = P(None, "win", "seq", None)

    return jax.shard_map(
        on_device,
        mesh=mesh,
        in_specs=(spec,) * 4,
        out_specs=(spec,) * 3,
        check_vma=False,
    )
```

```python
import functools
import math

import jax
import jax.numpy as jnp
from jax import lax
from jax.experimental import pallas as pl
from jax.experimental.pallas import tpu as pltpu
from jax.sharding import PartitionSpec as P


HDIM = 128
COLS = 64
HALF = COLS // 2
UNITS = 2


def exchanged(block, across, west):
    wins, seqs = lax.axis_size("win"), lax.axis_size("seq")
    route = [
        (w * seqs + s, ((w - west) % wins) * seqs + (s ^ across))
        for w in range(wins)
        for s in range(seqs)
    ]
    return lax.ppermute(block, ("win", "seq"), route)


def cost(flops, read, exps=0):
    return pl.CostEstimate(flops=int(flops), bytes_accessed=int(read), transcendentals=int(exps))


def packed(arrays, me, sample, first, units, heads_each, peers):
    rows = arrays[0][0].shape[2]
    width = units * HDIM
    share, offset = heads_each // units, first // units
    sizes = [rows * (COLS if half is None else HALF) for _, half in arrays]
    count = len(arrays)

    def kernel(me_ref, *refs):
        for i in range(len(peers)):
            out, at = refs[i - len(peers)], 0
            for piece, size in zip(refs[i * count :], sizes):
                out[at : at + size] = piece[0, 0].reshape(size, width)
                at += size

    specs = [
        pl.BlockSpec(
            (1, 1, rows, COLS if half is None else HALF, width),
            lambda u, m, k=k, half=half: (sample, 0, 0, half or 0, (m[0] ^ k) * share + offset),
        )
        for k in peers
        for _, half in arrays
    ]
    out = pl.pallas_call(
        kernel,
        grid_spec=pltpu.PrefetchScalarGridSpec(
            num_scalar_prefetch=1,
            grid=(1,),
            in_specs=specs,
            out_specs=[pl.BlockSpec((sum(sizes), width), lambda u, m: (0, 0))] * len(peers),
        ),
        out_shape=[jax.ShapeDtypeStruct((sum(sizes), width), jnp.bfloat16)] * len(peers),
        name="pack",
        cost_estimate=cost(0, 4 * sum(sizes) * width * len(peers)),
    )(me, *[a for _ in peers for a, _ in arrays])
    return dict(zip(peers, out))


def window_grads(args, me, sample, first, units, heads_each, seqs, arrived, arrived_west):
    rows = args[0].shape[2]
    tokens, part = rows * COLS, rows * HALF
    total = tokens * seqs
    block, slab = min(512, total), min(256, total)
    turned = seqs // 2
    here = [k for k in range(seqs) if k]
    factor = HDIM ** (-0.5)
    slope = factor * math.log2(math.e)

    def product(a, b, i, j):
        return lax.dot_general(a, b, (((i,), (j,)), ((), ())), preferred_element_type=jnp.float32)

    def folded(reduce, x):
        return reduce(x.reshape(-1, 8, x.shape[1]), axis=0)

    def kernel(me_ref, q_own, k_own, v_own, g_own, *refs):
        got = refs[: len(here)]
        got_west = refs[len(here) : len(here) + seqs]
        outs = refs[-8 - 2 * seqs : -8]
        qs, ks, vs, gs, kt, dq, dk, dv = refs[-8:]

        for n, (own, held) in enumerate(((q_own, qs), (k_own, ks), (v_own, vs))):
            held[0:tokens] = own[0, 0].reshape(tokens, HDIM)
            for i, k in enumerate(here):
                held[k * tokens : (k + 1) * tokens] = got[i][n * tokens : (n + 1) * tokens]
        for k in range(seqs):
            near = g_own[0, 0] if k == 0 else got[k - 1][3 * tokens :].reshape(rows, HALF, HDIM)
            far = got_west[k][...].reshape(rows, HALF, HDIM)
            at = (k ^ turned) * tokens
            gs[at : at + tokens] = jnp.concatenate([near, far], axis=1).reshape(tokens, HDIM)
        kt[...] = ks[...].T
        dk[...] = jnp.zeros_like(dk)
        dv[...] = jnp.zeros_like(dv)

        def step(i, carry):
            at = pl.ds(pl.multiple_of(i * block, block), block)
            query, grad = qs[at, :], gs[at, :]
            slabs = [slice(j, j + slab) for j in range(0, total, slab)]
            scores = [product(ks[j, :], query, 1, 1) for j in slabs]
            top = functools.reduce(jnp.maximum, [folded(jnp.max, x) for x in scores])
            top = jnp.max(top, axis=0, keepdims=True) * slope
            weights = [jnp.exp2(x * slope - top) for x in scores]
            grad_probs = [product(vs[j, :], grad, 1, 1) for j in slabs]
            mass = sum(folded(jnp.sum, w) for w in weights)
            dots = sum(folded(jnp.sum, w * g) for w, g in zip(weights, grad_probs))
            scale = 1.0 / jnp.sum(mass, axis=0, keepdims=True)
            row_dot = jnp.sum(dots, axis=0, keepdims=True) * scale
            column = scale.T
            grad = (grad.astype(jnp.float32) * column).astype(jnp.bfloat16)
            query = (query.astype(jnp.float32) * (column * factor)).astype(jnp.bfloat16)
            turned_grad = 0.0
            for j, w, g in zip(slabs, weights, grad_probs):
                dv[j, :] += product(w.astype(jnp.bfloat16), grad, 1, 0)
                u = (w * (g - row_dot)).astype(jnp.bfloat16)
                dk[j, :] += product(u, query, 1, 0)
                turned_grad += product(kt[:, j], u, 1, 0)
            dq[at, :] = (turned_grad * (scale * factor)).T.astype(jnp.bfloat16)
            return carry

        lax.fori_loop(0, total // block, step, 0)

        for k in range(seqs):
            at = pl.ds((k ^ turned) * tokens, tokens)
            for n, held in enumerate((dq, dk, dv)):
                value = held[at, :]
                value = value.astype(jnp.bfloat16).reshape(rows, COLS, HDIM)
                to = pl.ds(n * part, part)
                outs[k][to, :] = value[:, :HALF].reshape(part, HDIM)
                outs[seqs + k][to, :] = value[:, HALF:].reshape(part, HDIM)

    own = [
        pl.BlockSpec(
            (1, 1, rows, COLS, HDIM), lambda u, m: (sample, 0, 0, 0, m[0] * heads_each + first + u)
        )
    ] * 3 + [
        pl.BlockSpec(
            (1, 1, rows, HALF, HDIM), lambda u, m: (sample, 0, 0, 1, m[0] * heads_each + first + u)
        )
    ]
    full, small = 3 * tokens + part, part
    got = [pl.BlockSpec((full, HDIM), lambda u, m: (0, u))] * len(here)
    got_west = [pl.BlockSpec((small, HDIM), lambda u, m: (0, first + u))] * seqs
    out_rows = 3 * part
    held = pltpu.VMEM((total, HDIM), jnp.bfloat16)
    wide = pltpu.VMEM((total, HDIM), jnp.float32)
    out = pl.pallas_call(
        kernel,
        grid_spec=pltpu.PrefetchScalarGridSpec(
            num_scalar_prefetch=1,
            grid=(units,),
            in_specs=own + got + got_west,
            out_specs=[pl.BlockSpec((out_rows, HDIM), lambda u, m: (0, u))] * (2 * seqs),
            scratch_shapes=[held] * 4
            + [pltpu.VMEM((HDIM, total), jnp.bfloat16), held, wide, wide],
        ),
        out_shape=[jax.ShapeDtypeStruct((out_rows, units * HDIM), jnp.bfloat16)] * (2 * seqs),
        compiler_params=pltpu.CompilerParams(vmem_limit_bytes=48 * 2**20),
        name="grads",
        cost_estimate=cost(
            units * 10 * total * total * HDIM, units * 14 * total * HDIM, units * total * total
        ),
    )(
        me,
        *args,
        *[arrived[k] for k in here],
        *[arrived_west[k] for k in range(seqs)],
    )
    return out[:seqs], out[seqs:]


def placed(results, me, shape, sample, first, units, heads_each, pieces, direct):
    rows = shape[2]
    width = units * HDIM
    share, offset = heads_each // units, first // units

    def kernel(me_ref, *refs):
        outs, sems = refs[-4:-1], refs[-1]
        copies = []
        for i, (k, column, _) in enumerate(pieces):
            head = pl.multiple_of(((me_ref[0] ^ k) * share + offset) * width, width)
            for n in range(3):
                to = outs[n].at[sample, 0, :, pl.ds(column, HALF), pl.ds(head, width)]
                copies.append(pltpu.make_async_copy(refs[i].at[n], to, sems.at[i, n]))
        for copy in copies:
            copy.start()
        for copy in copies:
            copy.wait()

    block = (3, rows, HALF, width)
    kept_spec = pl.BlockSpec(memory_space=pl.ANY)
    return pl.pallas_call(
        kernel,
        grid_spec=pltpu.PrefetchScalarGridSpec(
            num_scalar_prefetch=1,
            grid=(1,),
            in_specs=[kept_spec if direct else pl.BlockSpec(block, lambda k, m: (0, 0, 0, 0))]
            * len(pieces)
            + [kept_spec] * len(results),
            out_specs=[pl.BlockSpec(memory_space=pl.ANY)] * 3,
            scratch_shapes=[pltpu.SemaphoreType.DMA((len(pieces), 3))],
        ),
        out_shape=[jax.ShapeDtypeStruct(shape, jnp.bfloat16)] * 3,
        input_output_aliases={1 + len(pieces) + i: i for i in range(len(results))},
        compiler_params=pltpu.CompilerParams(vmem_limit_bytes=2**20) if direct else None,
        name="place",
        cost_estimate=cost(0, 4 * math.prod(block) * len(pieces)),
    )(me, *[x.reshape(block) for _, _, x in pieces], *results)


def on_device(*args):
    samples, _, local_tokens, model_width = args[0].shape
    seqs = lax.axis_size("seq")
    heads_each = model_width // HDIM // seqs
    rows = local_tokens // COLS
    me = lax.axis_index("seq").astype(jnp.int32).reshape(1)
    args = [a.reshape(samples, 1, rows, COLS, model_width) for a in args]
    shape = args[0].shape
    turned = seqs // 2
    crossing, beside = list(range(turned, seqs)), list(range(turned))
    units = math.gcd(UNITS, heads_each)
    chunks = [(n, f) for n in range(samples) for f in range(0, heads_each, units)]

    near = [(args[0], None), (args[1], None), (args[2], None), (args[3], 1)]
    moving, got_west, step = [], {}, 0

    def sent(arrays, place, peers, west):
        nonlocal step
        step += 1
        blocks = packed(arrays, me, *place, peers)
        return {k: exchanged(blocks[k], k, west) for k in peers}

    for sample, first in chunks:
        at = (sample, first, units, heads_each)
        got = {}
        if not moving:
            for k in crossing:
                got.update(sent(near, at, [k], 0))
        else:
            got.update(sent(near, at, crossing + beside[1:], 0))
        if sample not in got_west:
            whole = (sample, 0, heads_each, heads_each)
            got_west[sample] = sent([(args[3], 0)], whole, beside + crossing, 1)
        if not moving and beside[1:]:
            got.update(sent(near, at, beside[1:], 0))
        moving.append(got)
    leaving = []
    for (sample, first), got in zip(chunks, moving):
        stay, east = window_grads(
            args, me, sample, first, units, heads_each, seqs, got, got_west[sample]
        )
        came = {k: exchanged(east[k], k, -1) for k in crossing + beside}
        stayed = {k: exchanged(stay[k], k, 0) if k else stay[k] for k in crossing + beside}
        leaving.append((stayed, came))
    results = []
    for i, ((sample, first), (stayed, came)) in enumerate(zip(chunks, leaving)):
        early = [(k, HALF, stayed[k]) for k in beside] + [(k, 0, came[k]) for k in beside]
        late = [(k, 0, came[k]) for k in crossing]
        last = [(k, HALF, stayed[k]) for k in crossing]
        for pieces in [early, late, last] if i == len(chunks) - 1 else [early + late + last]:
            direct = pieces is late or pieces is last
            results = placed(
                results, me, shape, sample, first, units, heads_each, pieces, direct
            )
    return tuple(r.reshape(samples, 1, local_tokens, model_width) for r in results)


def solution(mesh):
    spec = P(None, "win", "seq", None)

    return jax.shard_map(
        on_device,
        mesh=mesh,
        in_specs=(spec,) * 4,
        out_specs=(spec,) * 3,
        check_vma=False,
    )
```

```python
import functools
import math

import jax
import jax.numpy as jnp
from jax import lax
from jax.experimental import pallas as pl
from jax.experimental.pallas import tpu as pltpu
from jax.sharding import PartitionSpec as P


HDIM = 128
COLS = 64
HALF = COLS // 2
UNITS = 2


def exchanged(block, across, west):
    wins, seqs = lax.axis_size("win"), lax.axis_size("seq")
    route = [
        (w * seqs + s, ((w - west) % wins) * seqs + (s ^ across))
        for w in range(wins)
        for s in range(seqs)
    ]
    return lax.ppermute(block, ("win", "seq"), route)


def cost(flops, read, exps=0):
    return pl.CostEstimate(flops=int(flops), bytes_accessed=int(read), transcendentals=int(exps))


def packed(arrays, me, sample, first, units, heads_each, peers):
    rows = arrays[0][0].shape[2]
    width = units * HDIM
    share, offset = heads_each // units, first // units
    sizes = [rows * (COLS if half is None else HALF) for _, half in arrays]
    count = len(arrays)

    def kernel(me_ref, *refs):
        for i in range(len(peers)):
            out, at = refs[i - len(peers)], 0
            for piece, size in zip(refs[i * count :], sizes):
                out[at : at + size] = piece[0, 0].reshape(size, width)
                at += size

    specs = [
        pl.BlockSpec(
            (1, 1, rows, COLS if half is None else HALF, width),
            lambda u, m, k=k, half=half: (sample, 0, 0, half or 0, (m[0] ^ k) * share + offset),
        )
        for k in peers
        for _, half in arrays
    ]
    out = pl.pallas_call(
        kernel,
        grid_spec=pltpu.PrefetchScalarGridSpec(
            num_scalar_prefetch=1,
            grid=(1,),
            in_specs=specs,
            out_specs=[pl.BlockSpec((sum(sizes), width), lambda u, m: (0, 0))] * len(peers),
        ),
        out_shape=[jax.ShapeDtypeStruct((sum(sizes), width), jnp.bfloat16)] * len(peers),
        name="pack",
        cost_estimate=cost(0, 4 * sum(sizes) * width * len(peers)),
    )(me, *[a for _ in peers for a, _ in arrays])
    return dict(zip(peers, out))


def packed_by_copies(arrays, me, sample, first, units, heads_each, peers):
    (peer,) = peers
    rows, model_width = arrays[0][0].shape[2], arrays[0][0].shape[4]
    width = units * HDIM
    share, offset = heads_each // units, first // units
    parts = COLS // HALF
    total = sum(rows * (parts if half is None else 1) for _, half in arrays)

    def kernel(me_ref, *refs):
        out, sems = refs[-2:]
        head = pl.multiple_of(((me_ref[0] ^ peer) * share + offset) * width, width)
        copies, at = [], 0
        for i, (_, half) in enumerate(arrays):
            size = rows * (parts if half is None else 1)
            lanes = pl.ds(head, width)
            if half is None:
                piece = refs[i].at[sample, :, :, lanes]
            else:
                piece = refs[i].at[sample, :, half, :, lanes]
            copies.append(pltpu.make_async_copy(piece, out.at[pl.ds(at, size)], sems.at[i]))
            at += size
        for copy in copies:
            copy.start()
        for copy in copies:
            copy.wait()

    samples = arrays[0][0].shape[0]
    views = [
        a.reshape((samples, rows * parts, HALF, model_width) if half is None
                  else (samples, rows, parts, HALF, model_width))
        for a, half in arrays
    ]
    anywhere = pl.BlockSpec(memory_space=pl.ANY)
    out = pl.pallas_call(
        kernel,
        grid_spec=pltpu.PrefetchScalarGridSpec(
            num_scalar_prefetch=1,
            grid=(1,),
            in_specs=[anywhere] * len(views),
            out_specs=anywhere,
            scratch_shapes=[pltpu.SemaphoreType.DMA((len(views),))],
        ),
        out_shape=jax.ShapeDtypeStruct((total, HALF, width), jnp.bfloat16),
        compiler_params=pltpu.CompilerParams(vmem_limit_bytes=2**20),
        name="pack",
        cost_estimate=cost(0, 4 * total * HALF * width),
    )(me, *views)
    return {peer: out.reshape(total * HALF, width)}


def window_grads(args, me, sample, first, units, heads_each, seqs, arrived, arrived_west):
    rows = args[0].shape[2]
    tokens, part = rows * COLS, rows * HALF
    total = tokens * seqs
    block, slab = min(512, total), min(256, total)
    turned = seqs // 2
    here = [k for k in range(seqs) if k]
    factor = HDIM ** (-0.5)
    slope = factor * math.log2(math.e)

    def product(a, b, i, j):
        return lax.dot_general(a, b, (((i,), (j,)), ((), ())), preferred_element_type=jnp.float32)

    def folded(reduce, x):
        return reduce(x.reshape(-1, 8, x.shape[1]), axis=0)

    def kernel(me_ref, q_own, k_own, v_own, g_own, *refs):
        got = refs[: len(here)]
        got_west = refs[len(here) : len(here) + seqs]
        outs = refs[-8 - 2 * seqs : -8]
        qs, ks, vs, gs, kt, dq, dk, dv = refs[-8:]

        for n, (own, held) in enumerate(((q_own, qs), (k_own, ks), (v_own, vs))):
            held[0:tokens] = own[0, 0].reshape(tokens, HDIM)
            for i, k in enumerate(here):
                held[k * tokens : (k + 1) * tokens] = got[i][n * tokens : (n + 1) * tokens]
        for k in range(seqs):
            near = g_own[0, 0] if k == 0 else got[k - 1][3 * tokens :].reshape(rows, HALF, HDIM)
            far = got_west[k][...].reshape(rows, HALF, HDIM)
            at = (k ^ turned) * tokens
            gs[at : at + tokens] = jnp.concatenate([near, far], axis=1).reshape(tokens, HDIM)
        kt[...] = ks[...].T
        dk[...] = jnp.zeros_like(dk)
        dv[...] = jnp.zeros_like(dv)

        def step(i, carry):
            at = pl.ds(pl.multiple_of(i * block, block), block)
            query, grad = qs[at, :], gs[at, :]
            slabs = [slice(j, j + slab) for j in range(0, total, slab)]
            scores = [product(ks[j, :], query, 1, 1) for j in slabs]
            top = functools.reduce(jnp.maximum, [folded(jnp.max, x) for x in scores])
            top = jnp.max(top, axis=0, keepdims=True) * slope
            weights = [jnp.exp2(x * slope - top) for x in scores]
            grad_probs = [product(vs[j, :], grad, 1, 1) for j in slabs]
            mass = sum(folded(jnp.sum, w) for w in weights)
            dots = sum(folded(jnp.sum, w * g) for w, g in zip(weights, grad_probs))
            scale = 1.0 / jnp.sum(mass, axis=0, keepdims=True)
            row_dot = jnp.sum(dots, axis=0, keepdims=True) * scale
            column = scale.T
            grad = (grad.astype(jnp.float32) * column).astype(jnp.bfloat16)
            query = (query.astype(jnp.float32) * (column * factor)).astype(jnp.bfloat16)
            turned_grad = 0.0
            for j, w, g in zip(slabs, weights, grad_probs):
                dv[j, :] += product(w.astype(jnp.bfloat16), grad, 1, 0)
                u = (w * (g - row_dot)).astype(jnp.bfloat16)
                dk[j, :] += product(u, query, 1, 0)
                turned_grad += product(kt[:, j], u, 1, 0)
            dq[at, :] = (turned_grad * (scale * factor)).T.astype(jnp.bfloat16)
            return carry

        lax.fori_loop(0, total // block, step, 0)

        for k in range(seqs):
            at = pl.ds((k ^ turned) * tokens, tokens)
            for n, held in enumerate((dq, dk, dv)):
                value = held[at, :]
                value = value.astype(jnp.bfloat16).reshape(rows, COLS, HDIM)
                to = pl.ds(n * part, part)
                outs[k][to, :] = value[:, :HALF].reshape(part, HDIM)
                outs[seqs + k][to, :] = value[:, HALF:].reshape(part, HDIM)

    own = [
        pl.BlockSpec(
            (1, 1, rows, COLS, HDIM), lambda u, m: (sample, 0, 0, 0, m[0] * heads_each + first + u)
        )
    ] * 3 + [
        pl.BlockSpec(
            (1, 1, rows, HALF, HDIM), lambda u, m: (sample, 0, 0, 1, m[0] * heads_each + first + u)
        )
    ]
    full, small = 3 * tokens + part, part
    got = [pl.BlockSpec((full, HDIM), lambda u, m: (0, u))] * len(here)
    got_west = [pl.BlockSpec((small, HDIM), lambda u, m: (0, first + u))] * seqs
    out_rows = 3 * part
    held = pltpu.VMEM((total, HDIM), jnp.bfloat16)
    wide = pltpu.VMEM((total, HDIM), jnp.float32)
    out = pl.pallas_call(
        kernel,
        grid_spec=pltpu.PrefetchScalarGridSpec(
            num_scalar_prefetch=1,
            grid=(units,),
            in_specs=own + got + got_west,
            out_specs=[pl.BlockSpec((out_rows, HDIM), lambda u, m: (0, u))] * (2 * seqs),
            scratch_shapes=[held] * 4
            + [pltpu.VMEM((HDIM, total), jnp.bfloat16), held, wide, wide],
        ),
        out_shape=[jax.ShapeDtypeStruct((out_rows, units * HDIM), jnp.bfloat16)] * (2 * seqs),
        compiler_params=pltpu.CompilerParams(vmem_limit_bytes=48 * 2**20),
        name="grads",
        cost_estimate=cost(
            units * 10 * total * total * HDIM, units * 14 * total * HDIM, units * total * total
        ),
    )(
        me,
        *args,
        *[arrived[k] for k in here],
        *[arrived_west[k] for k in range(seqs)],
    )
    return out[:seqs], out[seqs:]


def placed(results, me, shape, sample, first, units, heads_each, pieces, direct):
    rows = shape[2]
    width = units * HDIM
    share, offset = heads_each // units, first // units

    def kernel(me_ref, *refs):
        outs, sems = refs[-4:-1], refs[-1]
        copies = []
        for i, (k, column, _) in enumerate(pieces):
            head = pl.multiple_of(((me_ref[0] ^ k) * share + offset) * width, width)
            for n in range(3):
                to = outs[n].at[sample, 0, :, pl.ds(column, HALF), pl.ds(head, width)]
                copies.append(pltpu.make_async_copy(refs[i].at[n], to, sems.at[i, n]))
        for copy in copies:
            copy.start()
        for copy in copies:
            copy.wait()

    block = (3, rows, HALF, width)
    kept_spec = pl.BlockSpec(memory_space=pl.ANY)
    return pl.pallas_call(
        kernel,
        grid_spec=pltpu.PrefetchScalarGridSpec(
            num_scalar_prefetch=1,
            grid=(1,),
            in_specs=[kept_spec if direct else pl.BlockSpec(block, lambda k, m: (0, 0, 0, 0))]
            * len(pieces)
            + [kept_spec] * len(results),
            out_specs=[pl.BlockSpec(memory_space=pl.ANY)] * 3,
            scratch_shapes=[pltpu.SemaphoreType.DMA((len(pieces), 3))],
        ),
        out_shape=[jax.ShapeDtypeStruct(shape, jnp.bfloat16)] * 3,
        input_output_aliases={1 + len(pieces) + i: i for i in range(len(results))},
        compiler_params=pltpu.CompilerParams(vmem_limit_bytes=2**20) if direct else None,
        name="place",
        cost_estimate=cost(0, 4 * math.prod(block) * len(pieces)),
    )(me, *[x.reshape(block) for _, _, x in pieces], *results)


def on_device(*args):
    samples, _, local_tokens, model_width = args[0].shape
    seqs = lax.axis_size("seq")
    heads_each = model_width // HDIM // seqs
    rows = local_tokens // COLS
    me = lax.axis_index("seq").astype(jnp.int32).reshape(1)
    args = [a.reshape(samples, 1, rows, COLS, model_width) for a in args]
    shape = args[0].shape
    turned = seqs // 2
    crossing, beside = list(range(turned, seqs)), list(range(turned))
    units = math.gcd(UNITS, heads_each)
    chunks = [(n, f) for n in range(samples) for f in range(0, heads_each, units)]

    near = [(args[0], None), (args[1], None), (args[2], None), (args[3], 1)]
    moving, got_west, step = [], {}, 0

    def sent(arrays, place, peers, west):
        nonlocal step
        step += 1
        pack = packed_by_copies if step == 1 else packed
        blocks = pack(arrays, me, *place, peers)
        return {k: exchanged(blocks[k], k, west) for k in peers}

    for sample, first in chunks:
        at = (sample, first, units, heads_each)
        got = {}
        if not moving:
            for k in crossing:
                got.update(sent(near, at, [k], 0))
        else:
            got.update(sent(near, at, crossing + beside[1:], 0))
        if sample not in got_west:
            whole = (sample, 0, heads_each, heads_each)
            got_west[sample] = sent([(args[3], 0)], whole, beside + crossing, 1)
        if not moving and beside[1:]:
            got.update(sent(near, at, beside[1:], 0))
        moving.append(got)
    leaving = []
    for (sample, first), got in zip(chunks, moving):
        stay, east = window_grads(
            args, me, sample, first, units, heads_each, seqs, got, got_west[sample]
        )
        came = {k: exchanged(east[k], k, -1) for k in crossing + beside}
        stayed = {k: exchanged(stay[k], k, 0) if k else stay[k] for k in crossing + beside}
        leaving.append((stayed, came))
    results = []
    for i, ((sample, first), (stayed, came)) in enumerate(zip(chunks, leaving)):
        early = [(k, HALF, stayed[k]) for k in beside] + [(k, 0, came[k]) for k in beside]
        late = [(k, 0, came[k]) for k in crossing]
        last = [(k, HALF, stayed[k]) for k in crossing]
        for pieces in [early, late, last] if i == len(chunks) - 1 else [early + late + last]:
            direct = pieces is late or pieces is last
            results = placed(
                results, me, shape, sample, first, units, heads_each, pieces, direct
            )
    return tuple(r.reshape(samples, 1, local_tokens, model_width) for r in results)


def solution(mesh):
    spec = P(None, "win", "seq", None)

    return jax.shard_map(
        on_device,
        mesh=mesh,
        in_specs=(spec,) * 4,
        out_specs=(spec,) * 3,
        check_vma=False,
    )
```
